32 devices in a mesh: dp: 32 (over z, y, x, core).
Axes of the slice: x: 2, y: 2, z: 4, core: 2. Of those that a mesh axis runs over, the one named last changes fastest.
Arguments:
- tokens: bfloat16 [4096, 1024], P('dp'), may hold values from -6 to 6
- lengths: int32 [32, 2], P('dp'), may hold values from 1 to 64, as said below
- cotangent: bfloat16 [4096, 1024], P('dp'), may hold values from -6 to 6
- norm1_gain: bfloat16 [1024], P('dp'), may hold values from 0.5 to 1.5
- norm1_shift: bfloat16 [1024], P('dp'), may hold values from -3 to 3
- joint_weight: bfloat16 [1024, 3072], P('dp'), may hold values from -0.1875 to 0.1875
- query_bias: bfloat16 [1024], P('dp'), may hold values from -3 to 3
- value_bias: bfloat16 [1024], P('dp'), may hold values from -3 to 3
- output_weight: bfloat16 [1024, 1024], P('dp'), may hold values from -0.5 to 0.5
- output_bias: bfloat16 [1024], P('dp'), may hold values from -3 to 3
- norm2_gain: bfloat16 [1024], P('dp'), may hold values from 0.5 to 1.5
- norm2_shift: bfloat16 [1024], P('dp'), may hold values from -3 to 3
- expand_weight: bfloat16 [1024, 4096], P('dp'), may hold values from -0.1875 to 0.1875
- expand_bias: bfloat16 [4096], P('dp'), may hold values from -3 to 3
- reduce_weight: bfloat16 [4096, 1024], P('dp'), may hold values from -0.09375 to 0.09375
- reduce_bias: bfloat16 [1024], P('dp'), may hold values from -3 to 3
Outputs:
- layer_output: bfloat16 [4096, 1024], P('dp')
- grad_tokens: float32 [4096, 1024], P('dp')
- grad_norm1_gain: float32 [1024], P('dp')
- grad_norm1_shift: float32 [1024], P('dp')
- grad_joint_weight: float32 [1024, 3072], P('dp')
- grad_query_bias: float32 [1024], P('dp')
- grad_value_bias: float32 [1024], P('dp')
- grad_output_weight: float32 [1024, 1024], P('dp')
- grad_output_bias: float32 [1024], P('dp')
- grad_norm2_gain: float32 [1024], P('dp')
- grad_norm2_shift: float32 [1024], P('dp')
- grad_expand_weight: float32 [1024, 4096], P('dp')
- grad_expand_bias: float32 [4096], P('dp')
- grad_reduce_weight: float32 [4096, 1024], P('dp')
- grad_reduce_bias: float32 [1024], P('dp')
The draws below stay inside these ranges and needn't reach their ends.
Inputs may be any that keep to these rules, and one draw needn't show every extreme that they name: On every device one sequence has the largest length 64, and on one device all sequences have it; the lengths of a device sum to at most 128.
All inputs are finite; a program needn't handle non-finite values.
Results may differ from the reference program's by a relative error of at most 0.011.
Values may be sent and summed in bfloat16 or wider, within the bound.
A program may use at most 192 MiB of HBM per device.

```python
import jax
import jax.numpy as jnp
from jax import lax

D = 1024
HEADS = 16
FF = 4096
ROWS = 128
SEQS_DEV = 2
GROUPS = 32
TOKENS = 4096


def draw_lengths(key, part):
    first_key = jax.random.fold_in(key, 11)
    pick_key = jax.random.fold_in(key, 23)
    full_key = jax.random.fold_in(key, 37)
    longest = ROWS // SEQS_DEV
    drawn = jax.random.randint(first_key, (GROUPS, SEQS_DEV), 1, longest + 1)
    picked = jax.random.randint(pick_key, (GROUPS, 1), 0, SEQS_DEV)
    column = jnp.arange(SEQS_DEV, dtype=jnp.int32)[None, :]
    drawn = jnp.where(column == picked, longest, drawn)
    chosen = jax.random.randint(full_key, (), 0, GROUPS)
    device_row = jnp.arange(GROUPS, dtype=jnp.int32)[:, None]
    drawn = jnp.where(device_row == chosen, longest, drawn)
    return drawn.astype(jnp.int32)


def levels(stream_key, extent, split, least, top_value):
    def one(dim, blocks):
        draws = jax.random.uniform(jax.random.fold_in(jax.random.fold_in(stream_key, 6), dim), (blocks,), jnp.float32, least / len(split), top_value / len(split))
        return jnp.repeat(jnp.exp(draws), extent[dim] // blocks).reshape((-1,) + (1,) * (len(extent) - dim - 1))

    loudness = one(*split[0])
    for cut in split[1:]:
        loudness = loudness * one(*cut)
    return loudness


def noise(key, extent, scale, most, pieces=(), held_as=jnp.bfloat16):
    loudness = levels(key, extent, pieces, -0.22, 0.18) if pieces else 1.0
    values = jax.random.normal(key, extent, jnp.float32) * scale * loudness
    return jnp.minimum(jnp.maximum(values, -most), most).astype(held_as)


def setup_inputs(seed: int = 0) -> dict:
    arg_keys = jax.random.split(jax.random.key(seed), 17)
    return {
        "tokens": noise(arg_keys[0], (TOKENS, D), 1.0, 6.0, ((0, 32),)),
        "lengths": draw_lengths(jax.random.fold_in(arg_keys[16], 71), 0),
        "cotangent": noise(arg_keys[2], (TOKENS, D), 1.0, 6.0, ((0, 32),)),
        "norm1_gain": jnp.clip(1.0 + 0.1 * jax.random.normal(arg_keys[3], (D,), jnp.float32), 0.5, 1.5).astype(jnp.bfloat16),
        "norm1_shift": noise(arg_keys[4], (D,), 0.3, 3.0, ((0, 32),)),
        "joint_weight": noise(arg_keys[5], (D, 3 * D), D ** -0.5, 0.1875, ((0, 32),)),
        "query_bias": noise(arg_keys[6], (D,), 0.5, 3.0, ((0, 32),)),
        "value_bias": noise(arg_keys[7], (D,), 0.5, 3.0, ((0, 32),)),
        "output_weight": noise(arg_keys[8], (D, D), (D // 8) ** -0.5, 0.5, ((0, 32),)),
        "output_bias": noise(arg_keys[9], (D,), 0.5, 3.0, ((0, 32),)),
        "norm2_gain": jnp.clip(1.0 + 0.1 * jax.random.normal(arg_keys[10], (D,), jnp.float32), 0.5, 1.5).astype(jnp.bfloat16),
        "norm2_shift": noise(arg_keys[11], (D,), 0.3, 3.0, ((0, 32),)),
        "expand_weight": noise(arg_keys[12], (D, FF), D ** -0.5, 0.1875, ((0, 32),)),
        "expand_bias": noise(arg_keys[13], (FF,), 0.5, 3.0, ((0, 32),)),
        "reduce_weight": noise(arg_keys[14], (FF, D), FF ** -0.5, 0.09375, ((0, 32),)),
        "reduce_bias": noise(arg_keys[15], (D,), 0.5, 3.0, ((0, 32),)),
    }


EPSILON = 1e-05
TANH_SCALE = 0.7978845608028654
CUBIC_TERM = 0.044715

def layer_norm(row_data, gain_vector, shift_vector):
    average = lax.optimization_barrier(jnp.mean(row_data, axis=-1, keepdims=True))
    centred = row_data - average
    spread = lax.optimization_barrier(jnp.mean(centred * centred, axis=-1, keepdims=True))
    return centred * lax.rsqrt(spread + EPSILON) * gain_vector + shift_vector

def activation(values_in):
    return 0.5 * values_in * (1.0 + jnp.tanh(TANH_SCALE * (values_in + CUBIC_TERM * values_in * values_in * values_in)))

def contract(pattern, first_op, second_op):
    return jnp.einsum(pattern, first_op.astype(jnp.float32), second_op.astype(jnp.float32))

def transposed_left(first_op, second_op):
    return lax.dot_general(first_op, second_op, (((0,), (0,)), ((), ())), preferred_element_type=jnp.float32)

def transposed_right(first_op, second_op):
    return lax.dot_general(first_op, second_op, (((1,), (1,)), ((), ())), preferred_element_type=jnp.float32)

def slot_mask(lengths_row, row_count):
    seq_ends = jnp.cumsum(lengths_row).astype(jnp.int32)
    position = jnp.arange(row_count, dtype=jnp.int32)
    segment = lax.optimization_barrier(jnp.sum((position[:, None] >= seq_ends[None, :]).astype(jnp.int32), axis=1)).astype(jnp.int32)
    live_rows = position < seq_ends[-1]
    segment = jnp.where(live_rows, segment, row_count + position)
    allowed = (segment[:, None] == segment[None, :]) & (position[:, None] >= position[None, :])
    return (allowed, live_rows.astype(jnp.float32))

def masked_scores(query_heads, key_heads, allowed):
    score_scale = query_heads.shape[2] ** (-0.5)
    scores = contract('qhd,khd->hqk', query_heads, key_heads) * score_scale
    return jnp.where(allowed[None, :, :], scores, -1e+30)

def forward(tokens, lengths_row, attn_params, ffn_params):
    gain_first, shift_first, joint_weight, query_bias, value_bias, output_weight, output_bias = attn_params
    gain_second, shift_second, expand_weight, expand_bias, reduce_weight, reduce_bias = ffn_params
    row_count, model_width = tokens.shape
    head_size = model_width // HEADS
    allowed, live_rows = slot_mask(lengths_row, row_count)
    residual = tokens.astype(jnp.float32)
    first_normed = layer_norm(residual, gain_first.astype(jnp.float32), shift_first.astype(jnp.float32)).astype(jnp.bfloat16)
    packed = jnp.dot(first_normed, joint_weight, preferred_element_type=jnp.float32)
    query_heads = (packed[:, :model_width] + query_bias.astype(jnp.float32)).astype(jnp.bfloat16).reshape(row_count, HEADS, head_size)
    key_heads = packed[:, model_width:2 * model_width].astype(jnp.bfloat16).reshape(row_count, HEADS, head_size)
    value_heads = (packed[:, 2 * model_width:] + value_bias.astype(jnp.float32)).astype(jnp.bfloat16).reshape(row_count, HEADS, head_size)
    scores = masked_scores(query_heads, key_heads, allowed)
    row_top = lax.optimization_barrier(jnp.max(scores, axis=-1, keepdims=True))
    logsum = row_top + jnp.log(lax.optimization_barrier(jnp.sum(jnp.exp(scores - row_top), axis=-1, keepdims=True)))
    weights = jnp.exp(scores - logsum).astype(jnp.bfloat16)
    context = contract('hqk,khd->qhd', weights, value_heads).astype(jnp.bfloat16).reshape(row_count, model_width)
    middle = residual + jnp.dot(context, output_weight, preferred_element_type=jnp.float32) + output_bias.astype(jnp.float32)
    second_normed = layer_norm(middle, gain_second.astype(jnp.float32), shift_second.astype(jnp.float32)).astype(jnp.bfloat16)
    before = jnp.dot(second_normed, expand_weight, preferred_element_type=jnp.float32) + expand_bias.astype(jnp.float32)
    active = activation(before).astype(jnp.bfloat16)
    block_final = middle + jnp.dot(active, reduce_weight, preferred_element_type=jnp.float32) + reduce_bias.astype(jnp.float32)
    stored_state = (residual, first_normed, query_heads, key_heads, value_heads, allowed, live_rows, logsum, context, middle, second_normed, before, active)
    return (block_final.astype(jnp.bfloat16), stored_state)

def backward(stored_state, cotangent, attn_params, ffn_params):
    residual, first_normed, query_heads, key_heads, value_heads, allowed, live_rows, logsum, context, middle, second_normed, before, active = stored_state
    gain_first, shift_first, joint_weight, query_bias, value_bias, output_weight, output_bias = attn_params
    gain_second, shift_second, expand_weight, expand_bias, reduce_weight, reduce_bias = ffn_params
    row_count, model_width = residual.shape
    head_size = model_width // HEADS
    score_scale = head_size ** (-0.5)
    grad_final = cotangent.astype(jnp.float32) * live_rows[:, None]
    grad_final_low = grad_final.astype(jnp.bfloat16)
    grad_reduce_bias = lax.optimization_barrier(jnp.sum(grad_final, axis=0))
    grad_reduce_weight = transposed_left(active, grad_final_low)
    grad_active = transposed_right(grad_final_low, reduce_weight)
    unused_value, curve_back = jax.vjp(activation, before)
    grad_before = curve_back(grad_active)[0]
    grad_expand_bias = lax.optimization_barrier(jnp.sum(grad_before, axis=0))
    grad_before_low = grad_before.astype(jnp.bfloat16)
    grad_expand_weight = transposed_left(second_normed, grad_before_low)
    grad_second_normed = transposed_right(grad_before_low, expand_weight)
    unused_norm, second_back = jax.vjp(layer_norm, middle, gain_second.astype(jnp.float32), shift_second.astype(jnp.float32))
    grad_middle_norm, grad_gain_second, grad_shift_second = second_back(grad_second_normed)
    grad_middle = grad_final + grad_middle_norm
    grad_middle_low = grad_middle.astype(jnp.bfloat16)
    grad_output_bias = lax.optimization_barrier(jnp.sum(grad_middle, axis=0))
    grad_output_weight = transposed_left(context, grad_middle_low)
    grad_context = transposed_right(grad_middle_low, output_weight).astype(jnp.bfloat16).reshape(row_count, HEADS, head_size)
    scores = masked_scores(query_heads, key_heads, allowed)
    probs = jnp.exp(scores - logsum)
    weights = probs.astype(jnp.bfloat16)
    grad_probs = contract('qhd,khd->hqk', grad_context, value_heads)
    grad_values = contract('hqk,qhd->khd', weights, grad_context)
    centre = lax.optimization_barrier(jnp.sum(probs * grad_probs, axis=-1, keepdims=True))
    grad_scores = (probs * (grad_probs - centre) * score_scale).astype(jnp.bfloat16)
    grad_query = contract('hqk,khd->qhd', grad_scores, key_heads).reshape(row_count, model_width)
    grad_keys = contract('hqk,qhd->khd', grad_scores, query_heads).reshape(row_count, model_width)
    grad_values = grad_values.reshape(row_count, model_width)
    grad_query_bias = lax.optimization_barrier(jnp.sum(grad_query, axis=0))
    grad_value_bias = lax.optimization_barrier(jnp.sum(grad_values, axis=0))
    grad_packed = jnp.concatenate([grad_query, grad_keys, grad_values], axis=1).astype(jnp.bfloat16)
    grad_joint_weight = transposed_left(first_normed, grad_packed)
    grad_first_normed = transposed_right(grad_packed, joint_weight)
    unused_first, first_back = jax.vjp(layer_norm, residual, gain_first.astype(jnp.float32), shift_first.astype(jnp.float32))
    grad_tokens_norm, grad_gain_first, grad_shift_first = first_back(grad_first_normed)
    grad_tokens = grad_middle + grad_tokens_norm
    attn_grads = (grad_gain_first, grad_shift_first, grad_joint_weight, grad_query_bias, grad_value_bias, grad_output_weight, grad_output_bias)
    ffn_grads = (grad_gain_second, grad_shift_second, grad_expand_weight, grad_expand_bias, grad_reduce_weight, grad_reduce_bias)
    return (grad_tokens, attn_grads, ffn_grads)

def reference(tokens, lengths, cotangent, norm1_gain, norm1_shift, joint_weight, query_bias, value_bias, output_weight, output_bias, norm2_gain, norm2_shift, expand_weight, expand_bias, reduce_weight, reduce_bias):
    attn_params = (norm1_gain, norm1_shift, joint_weight, query_bias, value_bias, output_weight, output_bias)
    ffn_params = (norm2_gain, norm2_shift, expand_weight, expand_bias, reduce_weight, reduce_bias)
    blocks_in = (tokens.reshape(GROUPS, ROWS, D), lengths, cotangent.reshape(GROUPS, ROWS, D))
    start_totals = jax.tree.map(lambda member: jnp.zeros(member.shape, jnp.float32), (attn_params, ffn_params))

    def step(totals, block_data):
        block_tokens, block_lengths, block_cotangent = block_data
        block_output, stored_state = forward(block_tokens, block_lengths, attn_params, ffn_params)
        grad_block, attn_grads, ffn_grads = backward(stored_state, block_cotangent, attn_params, ffn_params)
        totals = jax.tree.map(lambda first_op, second_op: first_op + second_op, totals, (attn_grads, ffn_grads))
        return (totals, (block_output, grad_block))
    final_totals, stacked = lax.scan(step, start_totals, blocks_in)
    attn_total, ffn_total = final_totals
    outputs_all, grads_all = stacked
    return (outputs_all.reshape(TOKENS, D), grads_all.reshape(TOKENS, D), attn_total[0], attn_total[1], attn_total[2], attn_total[3], attn_total[4], attn_total[5], attn_total[6], ffn_total[0], ffn_total[1], ffn_total[2], ffn_total[3], ffn_total[4], ffn_total[5])
```

```python
import jax
import jax.numpy as jnp
from jax import lax
from jax.sharding import PartitionSpec as P

HEADS = 16


EPSILON = 1e-05
TANH_SCALE = 0.7978845608028654
CUBIC_TERM = 0.044715


def layer_norm(row_data, gain_vector, shift_vector):
    average = jnp.mean(row_data, axis=-1, keepdims=True)
    centred = row_data - average
    spread = jnp.mean(centred * centred, axis=-1, keepdims=True)
    return centred * lax.rsqrt(spread + EPSILON) * gain_vector + shift_vector


def activation(values_in):
    return (
        0.5
        * values_in
        * (
            1.0
            + jnp.tanh(TANH_SCALE * (values_in + CUBIC_TERM * values_in * values_in * values_in))
        )
    )


def contract(pattern, first_op, second_op):
    return jnp.einsum(pattern, first_op, second_op, preferred_element_type=jnp.float32)


def transposed_left(first_op, second_op):
    return lax.dot_general(
        first_op, second_op, (((0,), (0,)), ((), ())), preferred_element_type=jnp.float32
    )


def transposed_right(first_op, second_op):
    return lax.dot_general(
        first_op, second_op, (((1,), (1,)), ((), ())), preferred_element_type=jnp.float32
    )


def slot_mask(lengths_row, row_count):
    seq_ends = jnp.cumsum(lengths_row)
    position = jnp.arange(row_count, dtype=jnp.int32)
    segment = jnp.sum((position[:, None] >= seq_ends[None, :]).astype(jnp.int32), axis=1)
    live_rows = position < seq_ends[-1]
    segment = jnp.where(live_rows, segment, row_count + position)
    allowed = (segment[:, None] == segment[None, :]) & (position[:, None] >= position[None, :])
    return (allowed, live_rows.astype(jnp.float32))


def masked_scores(query_heads, key_heads, allowed):
    score_scale = query_heads.shape[2] ** (-0.5)
    scores = contract("qhd,khd->hqk", query_heads, key_heads) * score_scale
    return jnp.where(allowed[None, :, :], scores, -1e30)


def forward(tokens, lengths_row, attn_params, ffn_params):
    gain_first, shift_first, joint_weight, query_bias, value_bias, output_weight, output_bias = (
        attn_params
    )
    gain_second, shift_second, expand_weight, expand_bias, reduce_weight, reduce_bias = ffn_params
    row_count, model_width = tokens.shape
    head_size = model_width // HEADS
    allowed, live_rows = slot_mask(lengths_row, row_count)
    residual = tokens.astype(jnp.float32)
    first_normed = layer_norm(
        residual, gain_first.astype(jnp.float32), shift_first.astype(jnp.float32)
    ).astype(jnp.bfloat16)
    packed = jnp.dot(first_normed, joint_weight, preferred_element_type=jnp.float32)
    query_heads = (
        (packed[:, :model_width] + query_bias.astype(jnp.float32))
        .astype(jnp.bfloat16)
        .reshape(row_count, HEADS, head_size)
    )
    key_heads = (
        packed[:, model_width : 2 * model_width]
        .astype(jnp.bfloat16)
        .reshape(row_count, HEADS, head_size)
    )
    value_heads = (
        (packed[:, 2 * model_width :] + value_bias.astype(jnp.float32))
        .astype(jnp.bfloat16)
        .reshape(row_count, HEADS, head_size)
    )
    scores = masked_scores(query_heads, key_heads, allowed)
    row_top = jnp.max(scores, axis=-1, keepdims=True)
    logsum = row_top + jnp.log(jnp.sum(jnp.exp(scores - row_top), axis=-1, keepdims=True))
    weights = jnp.exp(scores - logsum).astype(jnp.bfloat16)
    context = (
        contract("hqk,khd->qhd", weights, value_heads)
        .astype(jnp.bfloat16)
        .reshape(row_count, model_width)
    )
    middle = (
        residual
        + jnp.dot(context, output_weight, preferred_element_type=jnp.float32)
        + output_bias.astype(jnp.float32)
    )
    second_normed = layer_norm(
        middle, gain_second.astype(jnp.float32), shift_second.astype(jnp.float32)
    ).astype(jnp.bfloat16)
    before = jnp.dot(
        second_normed, expand_weight, preferred_element_type=jnp.float32
    ) + expand_bias.astype(jnp.float32)
    active = activation(before).astype(jnp.bfloat16)
    block_final = (
        middle
        + jnp.dot(active, reduce_weight, preferred_element_type=jnp.float32)
        + reduce_bias.astype(jnp.float32)
    )
    stored_state = (
        residual,
        first_normed,
        query_heads,
        key_heads,
        value_heads,
        allowed,
        live_rows,
        logsum,
        context,
        middle,
        second_normed,
        before,
        active,
    )
    return (block_final.astype(jnp.bfloat16), stored_state)


def backward(stored_state, cotangent, attn_params, ffn_params):
    (
        residual,
        first_normed,
        query_heads,
        key_heads,
        value_heads,
        allowed,
        live_rows,
        logsum,
        context,
        middle,
        second_normed,
        before,
        active,
    ) = stored_state
    gain_first, shift_first, joint_weight, query_bias, value_bias, output_weight, output_bias = (
        attn_params
    )
    gain_second, shift_second, expand_weight, expand_bias, reduce_weight, reduce_bias = ffn_params
    row_count, model_width = residual.shape
    head_size = model_width // HEADS
    score_scale = head_size ** (-0.5)
    grad_final = cotangent.astype(jnp.float32) * live_rows[:, None]
    grad_final_low = grad_final.astype(jnp.bfloat16)
    grad_reduce_bias = jnp.sum(grad_final, axis=0)
    grad_active = transposed_right(grad_final_low, reduce_weight)
    unused_value, curve_back = jax.vjp(activation, before)
    grad_before = curve_back(grad_active)[0]
    grad_expand_bias = jnp.sum(grad_before, axis=0)
    grad_before_low = grad_before.astype(jnp.bfloat16)
    grad_second_normed = transposed_right(grad_before_low, expand_weight)
    unused_norm, second_back = jax.vjp(
        layer_norm, middle, gain_second.astype(jnp.float32), shift_second.astype(jnp.float32)
    )
    grad_middle_norm, grad_gain_second, grad_shift_second = second_back(grad_second_normed)
    grad_middle = grad_final + grad_middle_norm
    grad_middle_low = grad_middle.astype(jnp.bfloat16)
    grad_output_bias = jnp.sum(grad_middle, axis=0)
    grad_context = (
        transposed_right(grad_middle_low, output_weight)
        .astype(jnp.bfloat16)
        .reshape(row_count, HEADS, head_size)
    )
    scores = masked_scores(query_heads, key_heads, allowed)
    probs = jnp.exp(scores - logsum)
    weights = probs.astype(jnp.bfloat16)
    grad_probs = contract("qhd,khd->hqk", grad_context, value_heads)
    grad_values = contract("hqk,qhd->khd", weights, grad_context)
    centre = jnp.sum(probs * grad_probs, axis=-1, keepdims=True)
    grad_scores = (probs * (grad_probs - centre) * score_scale).astype(jnp.bfloat16)
    grad_query = contract("hqk,khd->qhd", grad_scores, key_heads).reshape(row_count, model_width)
    grad_keys = contract("hqk,qhd->khd", grad_scores, query_heads).reshape(row_count, model_width)
    grad_values = grad_values.reshape(row_count, model_width)
    grad_query_bias = jnp.sum(grad_query, axis=0)
    grad_value_bias = jnp.sum(grad_values, axis=0)
    grad_packed = jnp.concatenate([grad_query, grad_keys, grad_values], axis=1).astype(jnp.bfloat16)
    grad_first_normed = transposed_right(grad_packed, joint_weight)
    unused_first, first_back = jax.vjp(
        layer_norm, residual, gain_first.astype(jnp.float32), shift_first.astype(jnp.float32)
    )
    grad_tokens_norm, grad_gain_first, grad_shift_first = first_back(grad_first_normed)
    grad_tokens = grad_middle + grad_tokens_norm
    ffn_factors = (second_normed, grad_before_low, active, grad_final_low)
    ffn_small = (grad_gain_second, grad_shift_second, grad_expand_bias, grad_reduce_bias)
    attn_factors = (first_normed, grad_packed, context, grad_middle_low)
    attn_small = (
        grad_gain_first,
        grad_shift_first,
        grad_query_bias,
        grad_value_bias,
        grad_output_bias,
    )
    return (grad_tokens, ffn_factors, ffn_small, attn_factors, attn_small)


def split_blocks(matrix, block_rows):
    return jnp.concatenate(
        [
            matrix[start : start + block_rows]
            for start in range(0, matrix.shape[0], block_rows)
        ],
        axis=1,
    )


def small_width(count, block_rows):
    return 128 * (-(-count // (block_rows * 128)))


def gather_params(matrices, vectors):
    block_rows = matrices[0].shape[0]
    lengths = [vector.shape[0] for vector in vectors]
    width = small_width(sum(lengths), block_rows)
    flat = jnp.concatenate(
        list(vectors) + [jnp.zeros((width * block_rows - sum(lengths),), vectors[0].dtype)]
    )
    packed = jnp.concatenate(list(matrices) + [flat.reshape(block_rows, width)], axis=1)
    whole = lax.all_gather(packed, "dp", axis=0, tiled=True)
    columns, at = [], 0
    for matrix in matrices:
        columns.append(whole[:, at : at + matrix.shape[1]])
        at += matrix.shape[1]
    small = whole[:, at:].reshape(-1, block_rows * width)
    pieces, at = [], 0
    for length in lengths:
        pieces.append(small[:, at : at + length].reshape(-1))
        at += length
    return columns, pieces


def scatter_sum(matrices, vectors):
    low = [matrix.astype(jnp.bfloat16) for matrix in matrices]
    devices = lax.axis_size("dp")
    block_rows = matrices[0].shape[0] // devices
    lengths = [vector.shape[0] // devices for vector in vectors]
    if vectors:
        width = small_width(sum(lengths), block_rows)
        flat = jnp.concatenate(
            [vector.reshape(devices, -1) for vector in vectors]
            + [jnp.zeros((devices, width * block_rows - sum(lengths)), jnp.float32)],
            axis=1,
        )
        low.append(flat.astype(jnp.bfloat16).reshape(devices * block_rows, width))
    shard = lax.psum_scatter(
        jnp.concatenate(low, axis=1), "dp", scatter_dimension=0, tiled=True
    )
    columns, at = [], 0
    for matrix in matrices:
        columns.append(shard[:, at : at + matrix.shape[1]].astype(jnp.float32))
        at += matrix.shape[1]
    pieces = []
    if vectors:
        small, at = shard[:, at:].reshape(-1), 0
        for length in lengths:
            pieces.append(small[at : at + length].astype(jnp.float32))
            at += length
    return columns, pieces


def on_device(
    tokens,
    lengths,
    cotangent,
    norm1_gain,
    norm1_shift,
    joint_weight,
    query_bias,
    value_bias,
    output_weight,
    output_bias,
    norm2_gain,
    norm2_shift,
    expand_weight,
    expand_bias,
    reduce_weight,
    reduce_bias,
):
    model_width = tokens.shape[1]
    hidden_width = expand_weight.shape[1]
    devices = lax.axis_size("dp")
    block_rows = joint_weight.shape[0]
    blocks = reduce_weight.shape[0] // block_rows
    matrices, vectors = gather_params(
        (joint_weight, output_weight, expand_weight, split_blocks(reduce_weight, block_rows)),
        (
            norm1_gain,
            norm1_shift,
            query_bias,
            value_bias,
            output_bias,
            norm2_gain,
            norm2_shift,
            expand_bias,
            reduce_bias,
        ),
    )
    reduce_whole = (
        matrices[3]
        .reshape(devices, block_rows, blocks, model_width)
        .transpose(0, 2, 1, 3)
        .reshape(hidden_width, model_width)
    )
    attn_params = (
        vectors[0],
        vectors[1],
        matrices[0],
        vectors[2],
        vectors[3],
        matrices[1],
        vectors[4],
    )
    ffn_params = (vectors[5], vectors[6], matrices[2], vectors[7], reduce_whole, vectors[8])
    layer_output, stored_state = forward(tokens, lengths[0], attn_params, ffn_params)
    grad_tokens, ffn_factors, ffn_small, attn_factors, attn_small = backward(
        stored_state, cotangent, attn_params, ffn_params
    )
    second_normed, grad_before_low, active, grad_final_low = ffn_factors
    first_normed, grad_packed, context, grad_middle_low = attn_factors
    grad_reduce = (
        transposed_left(active, grad_final_low)
        .astype(jnp.bfloat16)
        .reshape(devices, blocks, block_rows, model_width)
        .transpose(0, 2, 1, 3)
        .reshape(devices * block_rows, blocks * model_width)
    )
    ffn_parts, unused_pieces = scatter_sum(
        (transposed_left(second_normed, grad_before_low), grad_reduce), ()
    )
    attn_parts, small_parts = scatter_sum(
        (
            transposed_left(first_normed, grad_packed),
            transposed_left(context, grad_middle_low),
        ),
        attn_small + ffn_small,
    )
    grad_reduce_shard = (
        ffn_parts[1]
        .reshape(block_rows, blocks, model_width)
        .transpose(1, 0, 2)
        .reshape(blocks * block_rows, model_width)
    )
    return (
        layer_output,
        grad_tokens,
        small_parts[0],
        small_parts[1],
        attn_parts[0],
        small_parts[2],
        small_parts[3],
        attn_parts[1],
        small_parts[4],
        small_parts[5],
        small_parts[6],
        ffn_parts[0],
        small_parts[7],
        grad_reduce_shard,
        small_parts[8],
    )


def solution(mesh):
    in_specs = (
        P("dp", None),
        P("dp", None),
        P("dp", None),
        P("dp"),
        P("dp"),
        P("dp", None),
        P("dp"),
        P("dp"),
        P("dp", None),
        P("dp"),
        P("dp"),
        P("dp"),
        P("dp", None),
        P("dp"),
        P("dp", None),
        P("dp"),
    )
    out_specs = (
        P("dp", None),
        P("dp", None),
        P("dp"),
        P("dp"),
        P("dp", None),
        P("dp"),
        P("dp"),
        P("dp", None),
        P("dp"),
        P("dp"),
        P("dp"),
        P("dp", None),
        P("dp"),
        P("dp", None),
        P("dp"),
    )
    return jax.shard_map(
        on_device, mesh=mesh, in_specs=in_specs, out_specs=out_specs, check_vma=False
    )
```
